32 devices in a mesh: col: 4 (over y, x), row: 8 (over z, core).
Axes of the slice: x: 2, y: 2, z: 4, core: 2. Of those that a mesh axis runs over, the one named last changes fastest.
Arguments:
- snapshots: bfloat16 [8192, 4096], P('row', 'col'), may hold values from -54 to 54
- rotations: bfloat16 [2, 4096, 1024], P(None, 'col'), may hold values from -1 to 2
Outputs:
- gram_first: float32 [4096, 1024], P(('col', 'row'))
- gram_second: float32 [4096, 1024], P(('col', 'row'))
- shrunk: bfloat16 [8192, 4096], P('row', 'col')
The draws below stay inside these ranges and needn't reach their ends.
All inputs are finite; a program needn't handle non-finite values.
Results may differ from the reference program's by a relative error of at most 0.012.
Values may be sent and summed in bfloat16 or wider, within the bound.
A program may use at most 64 MiB of HBM per device.

```python
import math
import jax
import jax.numpy as jnp
from jax import lax

BW = 512
ROWS_DEV = 1024
ROWS = 8192
COLS = 4096
N_COL = 4


def draw_snapshots(key, part):
    keys = jax.random.split(key, 6)
    positions = jnp.arange(ROWS, dtype=jnp.float32)
    width_rows = 1.2 * ROWS_DEV
    centres = jax.random.uniform(keys[5], (1, COLS), jnp.float32, 0.0, float(ROWS))
    offsets = (positions[:, None] - centres) / width_rows
    envelope = jnp.exp(-offsets * offsets) + 0.1
    mean_square = (width_rows * math.sqrt(math.pi / 2.0) + 0.2 * width_rows * math.sqrt(math.pi)) / ROWS + 0.01
    envelope = envelope / math.sqrt(mean_square)
    rough_rows = jax.random.uniform(keys[1], (ROWS, 1), jnp.float32, 0.75, 1.25)
    col_scale = jnp.exp(jax.random.uniform(keys[2], (1, COLS), jnp.float32, math.log(0.4), math.log(4.0)))
    values = jnp.clip(jax.random.normal(keys[0], (ROWS, COLS), jnp.float32), -4.0, 4.0)
    return jnp.clip(values * envelope * rough_rows * col_scale, -54.0, 54.0).astype(jnp.bfloat16)


def draw_rotations(key, part):
    width_pair = 2 * BW
    row_pos = jnp.arange(COLS) % width_pair
    identity = (row_pos[:, None] == jnp.arange(width_pair)[None, :]).astype(jnp.float32)
    noise = jnp.clip(jax.random.normal(key, (2, COLS, width_pair), jnp.float32), -4.0, 4.0)
    return (identity[None] + noise * (0.6 / math.sqrt(width_pair))).astype(jnp.bfloat16)


def setup_inputs(seed: int = 0) -> dict:
    seeds = jax.random.split(jax.random.key(seed), 3)
    snapshots = draw_snapshots(jax.random.fold_in(seeds[2], 71), 0)
    rotations = draw_rotations(jax.random.fold_in(seeds[2], 71), 0)
    return {"snapshots": snapshots, "rotations": rotations}


def gram_of(pair_cols):
    return lax.dot_general(pair_cols, pair_cols, (((0,), (0,)), ((), ())), preferred_element_type=jnp.float32) / ROWS

def first_step(inputs):
    pair_cols, rotation = inputs
    turned = jnp.dot(pair_cols, rotation, preferred_element_type=jnp.float32).astype(jnp.bfloat16)
    return (gram_of(pair_cols), turned)

def second_step(inputs):
    pair_cols, rotation = inputs
    moved = jnp.dot(pair_cols, rotation, preferred_element_type=jnp.float32)
    singular = jnp.sqrt(lax.optimization_barrier(jnp.sum(moved * moved, axis=0)) / ROWS + 1e-06)
    factor = jnp.maximum(singular - 1.8, 0.0) / singular
    return (gram_of(pair_cols), (moved * factor).astype(jnp.bfloat16))

def reference(snapshots, rotations):
    pairs = jnp.transpose(snapshots.reshape(ROWS, N_COL, 2 * BW), (1, 0, 2))
    rot_first = rotations[0].reshape(N_COL, 2 * BW, 2 * BW)
    rot_second = rotations[1].reshape(N_COL, 2 * BW, 2 * BW)
    gram_first, turned = lax.map(first_step, (pairs, rot_first))
    left_blocks = jnp.roll(turned[:, :, :BW], 1, axis=0)
    second_pairs = jnp.concatenate([left_blocks, turned[:, :, BW:]], axis=2)
    gram_second, shrunk = lax.map(second_step, (second_pairs, rot_second))
    return (gram_first.reshape(N_COL * 2 * BW, 2 * BW), gram_second.reshape(N_COL * 2 * BW, 2 * BW), jnp.transpose(shrunk, (1, 0, 2)).reshape(ROWS, N_COL * 2 * BW))
```

```python
import functools

import jax
import jax.numpy as jnp
from jax import lax
from jax.experimental import pallas as pl
from jax.experimental.pallas import tpu as pltpu
from jax.sharding import PartitionSpec as P

TILE = 256
LANE = 128


def kernel(
    n, n_col, x_hbm, rot_hbm, g1_hbm, g2_hbm, out_hbm,
    x, rot, left, pair, moved, part, peer, sums, landed, turn_out, turn_in,
    gram_out, energy, energy_in, shrunk,
    load_sem, left_send, left_recv, core_send, core_recv, z_send, z_recv,
    turn_send, turn_recv, e_send, e_recv, store_sem, shrunk_sem,
):
    rows, width = x.shape
    half = width // 2
    block = width // n
    groups = n // 2
    symmetric = block == LANE
    total_rows = rows * n
    tiles = width // TILE
    row_tiles = rows // TILE
    per_tile = TILE // (2 * block)
    turns = n // 2 - 1 if symmetric else 0

    me_col = lax.axis_index("col")
    me = lax.axis_index("row")
    core = lax.rem(me, 2)
    group = lax.div(me, 2)
    partner = me + 1 - 2 * core

    def peer_at(step):
        return lax.rem(me + step, n)

    load_x = pltpu.make_async_copy(x_hbm, x, load_sem.at[0])
    load_r0 = [
        pltpu.make_async_copy(
            rot_hbm.at[0, :, pl.ds(h * half, half)], rot.at[0, :, pl.ds(h * half, half)],
            load_sem.at[1 + h],
        )
        for h in range(2)
    ]
    load_r1 = pltpu.make_async_copy(rot_hbm.at[1], rot.at[1], load_sem.at[3])
    load_x.start()
    load_r0[0].start()
    load_r0[1].start()
    load_r1.start()

    following = lax.rem(me_col + 1, n_col)
    preceding = lax.rem(me_col + n_col - 1, n_col)
    barrier = pltpu.get_barrier_semaphore()
    for other in (following, preceding):
        pl.semaphore_signal(
            barrier, inc=1, device_id={"col": other, "row": me},
            device_id_type=pl.DeviceIdType.MESH,
        )
    for step in range(1, n):
        pl.semaphore_signal(
            barrier, inc=1, device_id={"col": me_col, "row": peer_at(step)},
            device_id_type=pl.DeviceIdType.MESH,
        )

    def remote(src, dst, send_sem, recv_sem, col, row):
        return pltpu.make_async_remote_copy(
            src_ref=src, dst_ref=dst, send_sem=send_sem, recv_sem=recv_sem,
            device_id={"col": col, "row": row}, device_id_type=pl.DeviceIdType.MESH,
        )

    def turn(into, first, column):
        def body(t, _):
            span = pl.ds(pl.multiple_of(t * TILE, TILE), TILE)
            into[span, pl.ds(column - first, TILE)] = jnp.dot(
                x[span, :], rot[0, :, pl.ds(column, TILE)], preferred_element_type=jnp.float32
            ).astype(jnp.bfloat16)
            return 0
        lax.fori_loop(0, row_tiles, body, 0)

    pieces = half // TILE
    left_copy = [
        remote(
            left.at[:, pl.ds(h * TILE, TILE)], pair.at[:, pl.ds(h * TILE, TILE)],
            left_send.at[h], left_recv.at[h], following, me,
        )
        for h in range(pieces)
    ]
    load_x.wait()
    load_r0[0].wait()
    for h in range(pieces):
        turn(left, 0, h * TILE)
        if h == 0:
            pl.semaphore_wait(barrier, n + 1)
        left_copy[h].start()

    def core_copy(s, q):
        span = pl.ds(q * per_tile, per_tile)
        return remote(
            part.at[s, 1 - core, span], peer.at[s, span],
            core_send.at[s, q], core_recv.at[s, q], me_col, partner,
        )

    def z_copy(s, k, g):
        return remote(
            sums.at[s, g], landed.at[s, k - 1], z_send.at[s, k - 1], z_recv.at[s, k - 1],
            me_col, 2 * g + core,
        )

    def gram_terms(s, source):
        def body(step, _):
            q = lax.rem(group + 1 + step, tiles) if symmetric else step
            columns = pl.ds(pl.multiple_of(q * TILE, TILE), TILE)
            flipped = source[:, columns].T
            for m in range(3 if symmetric else tiles):
                c = lax.rem(q + m, tiles) if symmetric else m
                term = jnp.dot(
                    flipped, source[:, pl.ds(pl.multiple_of(c * TILE, TILE), TILE)],
                    preferred_element_type=jnp.float32,
                ).astype(jnp.bfloat16)
                if symmetric:
                    lo = m * TILE
                    wide = TILE if m < 2 else LANE
                    part[s, 0, q, :, lo:lo + wide] = term[:LANE, :wide]
                    if m == 0:
                        part[s, 1, q, :, 0:LANE] = term[LANE:, LANE:]
                    else:
                        part[s, 1, q, :, lo - LANE:lo - LANE + TILE] = term[LANE:, :]
                else:
                    for e in range(2 * per_tile):
                        part[s, e % 2, q * per_tile + e // 2, :, m * TILE:(m + 1) * TILE] = term[
                            e * block:(e + 1) * block, :
                        ]
            core_copy(s, q).start()
            return 0
        lax.fori_loop(0, tiles, body, 0)

    def gram_pass(s):
        if not symmetric:
            for q in range(tiles):
                core_copy(s, q).wait_recv()
        def body(k, _):
            g = lax.rem(group + k, groups)
            if symmetric:
                core_copy(s, g).wait_recv()
            sums[s, g] = (
                part[s, core, g].astype(jnp.float32) + peer[s, g].astype(jnp.float32)
            ).astype(jnp.bfloat16)
            z_copy(s, k, g).start()
            return 0
        lax.fori_loop(1, groups, body, 0)

    def turn_copy(s, d):
        return remote(
            turn_out.at[s, d - 1], turn_in.at[s, d - 1],
            turn_send.at[s, d - 1], turn_recv.at[s, d - 1], me_col, peer_at(d),
        )

    def gram_sum(s):
        if symmetric:
            core_copy(s, group).wait_recv()
        for k in range(1, groups):
            z_copy(s, k, lax.rem(group + k, groups)).wait_recv()
        for d in range(part.shape[-1] // LANE):
            span = pl.ds(d * LANE, LANE)
            total = part[s, core, group, :, span].astype(jnp.float32) + peer[
                s, group, :, span
            ].astype(jnp.float32)
            for k in range(1, groups):
                total = total + landed[s, k - 1, :, span].astype(jnp.float32)
            total = total / total_rows
            if symmetric:
                if 1 <= d <= turns:
                    turn_out[s, d - 1] = total.T.astype(jnp.bfloat16)
                    turn_copy(s, d).start()
                at = pl.ds(pl.multiple_of(peer_at(d) * LANE, LANE), LANE)
                gram_out[s, :, at] = total
            else:
                gram_out[s, :, span] = total

    def gram_end(s, target):
        for d in range(1, turns + 1):
            turn_copy(s, d).wait_recv()
            at = pl.ds(pl.multiple_of(peer_at(n - d) * LANE, LANE), LANE)
            gram_out[s, :, at] = turn_in[s, d - 1].astype(jnp.float32)
        copy = pltpu.make_async_copy(gram_out.at[s], target, store_sem.at[s])
        copy.start()
        return copy

    gram_terms(0, x)
    load_r0[1].wait()
    for h in range(pieces):
        turn(pair, 0, half + h * TILE)
    gram_pass(0)

    load_r1.wait()

    def add_moved(first, depth, fresh):
        def body(t, acc):
            span = pl.ds(pl.multiple_of(t * TILE, TILE), TILE)
            value = jnp.dot(
                pair[span, pl.ds(first, depth)], rot[1, pl.ds(first, depth), :],
                preferred_element_type=jnp.float32,
            )
            if not fresh:
                value = value + moved[span, :]
            moved[span, :] = value
            return acc + jnp.sum(value * value, axis=0, keepdims=True)
        return lax.fori_loop(0, row_tiles, body, jnp.zeros((1, width), jnp.float32))

    add_moved(half, half, True)
    gram_sum(0)
    first_store = gram_end(0, g1_hbm)

    for h in range(pieces - 1):
        left_copy[h].wait_recv()
        add_moved(h * TILE, TILE, False)
    left_copy[pieces - 1].wait_recv()
    gram_terms(1, pair)
    energy[...] = add_moved(half - TILE, TILE, False)

    def e_copy(step):
        return remote(
            energy, energy_in.at[step - 1], e_send.at[step - 1], e_recv.at[step - 1],
            me_col, peer_at(step),
        )

    for step in range(1, n):
        e_copy(step).start()
    gram_pass(1)
    total = energy[...]
    for step in range(1, n):
        e_copy(step).wait_recv()
        total = total + energy_in[step - 1]
    singular = jnp.sqrt(total / total_rows + 1e-06)
    factor = jnp.maximum(singular - 1.8, 0.0) / singular

    def out_copy(t):
        span = pl.ds(pl.multiple_of(t * TILE, TILE), TILE)
        return pltpu.make_async_copy(shrunk.at[span, :], out_hbm.at[span, :], shrunk_sem.at[t])

    def shrink(t, _):
        span = pl.ds(pl.multiple_of(t * TILE, TILE), TILE)
        shrunk[span, :] = (moved[span, :] * factor).astype(jnp.bfloat16)
        out_copy(t).start()
        return 0

    lax.fori_loop(0, row_tiles, shrink, 0)
    gram_sum(1)
    second_store = gram_end(1, g2_hbm)

    for h in range(pieces):
        left_copy[h].wait_send()
    for s in range(2):
        for q in range(tiles):
            core_copy(s, q).wait_send()
        for k in range(1, groups):
            z_copy(s, k, lax.rem(group + k, groups)).wait_send()
        for d in range(1, turns + 1):
            turn_copy(s, d).wait_send()
    for step in range(1, n):
        e_copy(step).wait_send()
    for t in range(row_tiles):
        out_copy(t).wait()
    first_store.wait()
    second_store.wait()


def per_device(n, n_col, snapshots, rotations):
    rows, width = snapshots.shape
    half = width // 2
    block = width // n
    groups = n // 2
    tiles = width // TILE
    symmetric = block == LANE
    reach = (groups + 1) * LANE if symmetric else width
    turns = groups - 1 if symmetric else 1
    bf16, f32, dma = jnp.bfloat16, jnp.float32, pltpu.SemaphoreType.DMA
    anywhere = pl.BlockSpec(memory_space=pl.ANY)
    return pl.pallas_call(
        functools.partial(kernel, n, n_col),
        out_shape=(
            jax.ShapeDtypeStruct((block, width), f32),
            jax.ShapeDtypeStruct((block, width), f32),
            jax.ShapeDtypeStruct((rows, width), bf16),
        ),
        in_specs=[anywhere] * 2,
        out_specs=(anywhere,) * 3,
        scratch_shapes=[
            pltpu.VMEM((rows, width), bf16),
            pltpu.VMEM((2, width, width), bf16),
            pltpu.VMEM((rows, half), bf16),
            pltpu.VMEM((rows, width), bf16),
            pltpu.VMEM((rows, width), f32),
            pltpu.VMEM((2, 2, groups, block, reach), bf16),
            pltpu.VMEM((2, groups, block, reach), bf16),
            pltpu.VMEM((2, groups, block, reach), bf16),
            pltpu.VMEM((2, groups - 1, block, reach), bf16),
            pltpu.VMEM((2, turns, LANE, LANE), bf16),
            pltpu.VMEM((2, turns, LANE, LANE), bf16),
            pltpu.VMEM((2, block, width), f32),
            pltpu.VMEM((1, width), f32),
            pltpu.VMEM((n - 1, 1, width), f32),
            pltpu.VMEM((rows, width), bf16),
            dma((4,)),
            dma((half // TILE,)),
            dma((half // TILE,)),
            dma((2, tiles)),
            dma((2, tiles)),
            dma((2, groups - 1)),
            dma((2, groups - 1)),
            dma((2, turns)),
            dma((2, turns)),
            dma((n - 1,)),
            dma((n - 1,)),
            dma((2,)),
            dma((rows // TILE,)),
        ],
        compiler_params=pltpu.CompilerParams(
            collective_id=0, has_side_effects=True, vmem_limit_bytes=56 * 1024 * 1024
        ),
    )(snapshots, rotations)


def solution(mesh):
    return jax.shard_map(
        functools.partial(per_device, mesh.shape["row"], mesh.shape["col"]),
        mesh=mesh,
        in_specs=(P("row", "col"), P(None, "col", None)),
        out_specs=(P(("col", "row"), None), P(("col", "row"), None), P("row", "col")),
        check_vma=False,
    )
```

```python
import functools

import jax
import jax.numpy as jnp
from jax import lax
from jax.experimental import pallas as pl
from jax.experimental.pallas import tpu as pltpu
from jax.sharding import PartitionSpec as P

TILE = 256
LANE = 128

UNITS = ((0, 0), (0, 2), (0, 3), (0, 1), (2, 2), (2, 3), (2, 1), (3, 3), (3, 1), (1, 1))
FIRST = (0, 1, 2, 3, 4, 5, 6, 7, 8, 9)
STAGES = ((4, 5, 7), (0, 1, 2), (3, 6, 8, 9))


def kernel(
    n, n_col, x_hbm, rot_hbm, g1_hbm, g2_hbm, out_hbm,
    x, rot, left, pair, moved, part, peer, sums, landed, turn_out, turn_in,
    gram_out, energy, energy_in, shrunk,
    flipped, load_sem, left_send, left_recv, core_send, core_recv, z_send, z_recv,
    turn_send, turn_recv, e_send, e_recv, store_sem, shrunk_sem,
):
    rows, width = x.shape
    half = width // 2
    block = width // n
    groups = n // 2
    symmetric = n == 8 and block == LANE
    total_rows = rows * n
    tiles = width // TILE
    row_tiles = rows // TILE
    per_tile = TILE // (2 * block)

    me_col = lax.axis_index("col")
    me = lax.axis_index("row")
    core = lax.rem(me, 2)
    group = lax.div(me, 2)
    partner = me + 1 - 2 * core

    def peer_at(step):
        return lax.rem(me + step, n)

    load_x = pltpu.make_async_copy(x_hbm, x, load_sem.at[0])
    load_r0 = [
        pltpu.make_async_copy(
            rot_hbm.at[0, :, pl.ds(h * half, half)], rot.at[0, :, pl.ds(h * half, half)],
            load_sem.at[1 + h],
        )
        for h in range(2)
    ]
    load_r1 = pltpu.make_async_copy(rot_hbm.at[1], rot.at[1], load_sem.at[3])
    load_x.start()
    load_r0[0].start()
    load_r0[1].start()
    load_r1.start()

    following = lax.rem(me_col + 1, n_col)
    preceding = lax.rem(me_col + n_col - 1, n_col)
    barrier = pltpu.get_barrier_semaphore()
    for other in (following, preceding):
        pl.semaphore_signal(
            barrier, inc=1, device_id={"col": other, "row": me},
            device_id_type=pl.DeviceIdType.MESH,
        )
    for step in range(1, n):
        pl.semaphore_signal(
            barrier, inc=1, device_id={"col": me_col, "row": peer_at(step)},
            device_id_type=pl.DeviceIdType.MESH,
        )

    def remote(src, dst, send_sem, recv_sem, col, row):
        return pltpu.make_async_remote_copy(
            src_ref=src, dst_ref=dst, send_sem=send_sem, recv_sem=recv_sem,
            device_id={"col": col, "row": row}, device_id_type=pl.DeviceIdType.MESH,
        )

    def turn(into, first, column):
        def body(t, _):
            span = pl.ds(pl.multiple_of(t * TILE, TILE), TILE)
            into[span, pl.ds(column - first, TILE)] = jnp.dot(
                x[span, :], rot[0, :, pl.ds(column, TILE)], preferred_element_type=jnp.float32
            ).astype(jnp.bfloat16)
            return 0
        lax.fori_loop(0, row_tiles, body, 0)

    pieces = half // TILE
    left_copy = [
        remote(
            left.at[:, pl.ds(h * TILE, TILE)], pair.at[:, pl.ds(h * TILE, TILE)],
            left_send.at[h], left_recv.at[h], following, me,
        )
        for h in range(pieces)
    ]
    load_x.wait()
    load_r0[0].wait()
    for h in range(pieces):
        turn(left, 0, h * TILE)
        if h == 0:
            pl.semaphore_wait(barrier, n + 1)
        left_copy[h].start()

    def owned(u):
        g = UNITS[u][0]
        return [v for v in range(len(UNITS)) if UNITS[v][0] == g].index(u)

    def core_copy(s, u):
        return remote(
            part.at[s, 1 - core, u], peer.at[s, u],
            core_send.at[s, u], core_recv.at[s, u], me_col, partner,
        )

    def z_copy(s, u):
        g = UNITS[u][0] if symmetric else lax.rem(group + u, groups)
        k = lax.rem(g - group + 2 * groups - 1, groups)
        if symmetric:
            v = owned(u)
            return remote(
                sums.at[s, u], landed.at[s, v, k], z_send.at[s, u], z_recv.at[s, v, k],
                me_col, 2 * g + core,
            )
        return remote(
            sums.at[s, g], landed.at[s, 0, k], z_send.at[s, k], z_recv.at[s, 0, k],
            me_col, 2 * g + core,
        )

    def added(s, u):
        return part[s, core, u].astype(jnp.float32) + peer[s, u].astype(jnp.float32)

    def turn_copy(s, u, e):
        g, c = UNITS[u]
        return remote(
            turn_out.at[s, owned(u), e], turn_in.at[s, g, core],
            turn_send.at[s, owned(u), e], turn_recv.at[s, g, core], me_col, 2 * c + e,
        )

    def flip(source, g):
        flipped[g] = source[:, g * TILE:(g + 1) * TILE].T

    def pair_terms(s, source, units):
        for u in units:
            g, c = UNITS[u]
            term = jnp.dot(
                flipped[g], source[:, c * TILE:(c + 1) * TILE],
                preferred_element_type=jnp.float32,
            ).astype(jnp.bfloat16)
            part[s, 0, u] = term[:LANE]
            part[s, 1, u] = term[LANE:]
            core_copy(s, u).start()

    def pair_pass(s, units):
        for u in units:
            core_copy(s, u).wait_recv()

            @pl.when(group != UNITS[u][0])
            def _():
                sums[s, u] = added(s, u).astype(jnp.bfloat16)
                z_copy(s, u).start()

    def pair_sum(s, units):
        for u in units:
            g, c = UNITS[u]

            @pl.when(group == g)
            def _():
                v = owned(u)
                total = added(s, u)
                for k in range(groups - 1):
                    remote(
                        sums.at[s, u], landed.at[s, v, k], z_send.at[s, u], z_recv.at[s, v, k],
                        me_col, partner,
                    ).wait_recv()
                    total = total + landed[s, v, k].astype(jnp.float32)
                total = total / total_rows
                if c != g:
                    for e in range(2):
                        turn_out[s, v, e] = total[:, e * LANE:(e + 1) * LANE].T.astype(jnp.bfloat16)
                        turn_copy(s, u, e).start()
                gram_out[s, :, c * TILE:(c + 1) * TILE] = total

    def pair_turned(s, units):
        for u in units:
            g, c = UNITS[u]
            if c != g:

                @pl.when(group == c)
                def _():
                    for e in range(2):
                        remote(
                            turn_out.at[s, 0, 0], turn_in.at[s, g, e], turn_send.at[s, 0, 0],
                            turn_recv.at[s, g, e], me_col, partner,
                        ).wait_recv()
                        gram_out[s, :, (2 * g + e) * LANE:(2 * g + e + 1) * LANE] = turn_in[
                            s, g, e
                        ].astype(jnp.float32)

    def pair_drain(s, units):
        for u in units:
            g, c = UNITS[u]
            core_copy(s, u).wait_send()

            @pl.when(group != g)
            def _():
                z_copy(s, u).wait_send()

            if c != g:

                @pl.when(group == g)
                def _():
                    for e in range(2):
                        turn_copy(s, u, e).wait_send()

    def rows_copy(s, q):
        span = pl.ds(q * per_tile, per_tile)
        return remote(
            part.at[s, 1 - core, span], peer.at[s, span],
            core_send.at[s, q], core_recv.at[s, q], me_col, partner,
        )

    def rows_terms(s, source):
        def body(q, _):
            turned_tile = source[:, pl.ds(pl.multiple_of(q * TILE, TILE), TILE)].T
            for m in range(tiles):
                term = jnp.dot(
                    turned_tile, source[:, m * TILE:(m + 1) * TILE],
                    preferred_element_type=jnp.float32,
                ).astype(jnp.bfloat16)
                for e in range(2 * per_tile):
                    part[s, e % 2, q * per_tile + e // 2, :, m * TILE:(m + 1) * TILE] = term[
                        e * block:(e + 1) * block, :
                    ]
            rows_copy(s, q).start()
            return 0
        lax.fori_loop(0, tiles, body, 0)

    def rows_pass(s):
        for q in range(tiles):
            rows_copy(s, q).wait_recv()

        def body(k, _):
            g = lax.rem(group + k, groups)
            sums[s, g] = added(s, g).astype(jnp.bfloat16)
            z_copy(s, k).start()
            return 0
        lax.fori_loop(1, groups, body, 0)

    def rows_sum(s):
        total = added(s, group)
        for k in range(1, groups):
            z_copy(s, k).wait_recv()
            total = total + landed[s, 0, k - 1].astype(jnp.float32)
        gram_out[s] = total / total_rows

    def gram_store(s, target):
        return pltpu.make_async_copy(gram_out.at[s], target, store_sem.at[s])

    if symmetric:
        for g in range(tiles):
            flip(x, g)
            pair_terms(0, x, [u for u in FIRST if UNITS[u][0] == g])
    else:
        rows_terms(0, x)
    load_r0[1].wait()
    for h in range(pieces):
        turn(pair, 0, half + h * TILE)
    if symmetric:
        pair_pass(0, FIRST)
        flip(pair, 2)
        flip(pair, 3)
        pair_terms(1, pair, STAGES[0])
    else:
        rows_pass(0)

    load_r1.wait()

    def add_moved(first, depth, fresh):
        def body(t, acc):
            span = pl.ds(pl.multiple_of(t * TILE, TILE), TILE)
            value = jnp.dot(
                pair[span, pl.ds(first, depth)], rot[1, pl.ds(first, depth), :],
                preferred_element_type=jnp.float32,
            )
            if not fresh:
                value = value + moved[span, :]
            moved[span, :] = value
            return acc + jnp.sum(value * value, axis=0, keepdims=True)
        return lax.fori_loop(0, row_tiles, body, jnp.zeros((1, width), jnp.float32))

    add_moved(half, half, True)
    if symmetric:
        pair_pass(1, STAGES[0])
    left_copy[0].wait_recv()
    if symmetric:
        flip(pair, 0)
        pair_terms(1, pair, STAGES[1])
    for h in range(pieces - 1):
        if h > 0:
            left_copy[h].wait_recv()
        add_moved(h * TILE, TILE, False)
    if symmetric:
        pair_pass(1, STAGES[1])
        pair_sum(0, FIRST)
        pair_turned(0, FIRST)
    else:
        rows_sum(0)
    gram_store(0, g1_hbm).start()
    if symmetric:
        pair_sum(1, STAGES[0])
    left_copy[pieces - 1].wait_recv()
    if symmetric:
        flip(pair, 1)
        pair_terms(1, pair, STAGES[2])
    else:
        rows_terms(1, pair)
    energy[...] = add_moved(half - TILE, TILE, False)

    def e_copy(step):
        return remote(
            energy, energy_in.at[step - 1], e_send.at[step - 1], e_recv.at[step - 1],
            me_col, peer_at(step),
        )

    for step in range(1, n):
        e_copy(step).start()
    if symmetric:
        pair_pass(1, STAGES[2])
        pair_sum(1, STAGES[1])
        pair_turned(1, STAGES[0] + STAGES[1])
    else:
        rows_pass(1)
    total = energy[...]
    for step in range(1, n):
        e_copy(step).wait_recv()
        total = total + energy_in[step - 1]
    singular = jnp.sqrt(total / total_rows + 1e-06)
    factor = jnp.maximum(singular - 1.8, 0.0) / singular

    def out_copy(t):
        span = pl.ds(pl.multiple_of(t * TILE, TILE), TILE)
        return pltpu.make_async_copy(shrunk.at[span, :], out_hbm.at[span, :], shrunk_sem.at[t])

    def shrink(t, _):
        span = pl.ds(pl.multiple_of(t * TILE, TILE), TILE)
        shrunk[span, :] = (moved[span, :] * factor).astype(jnp.bfloat16)
        out_copy(t).start()
        return 0

    lax.fori_loop(0, row_tiles, shrink, 0)
    if symmetric:
        pair_sum(1, STAGES[2])
        pair_turned(1, STAGES[2])
    else:
        rows_sum(1)
    gram_store(1, g2_hbm).start()

    for h in range(pieces):
        left_copy[h].wait_send()
    for s in range(2):
        if symmetric:
            pair_drain(s, FIRST)
        else:
            for q in range(tiles):
                rows_copy(s, q).wait_send()
            for k in range(1, groups):
                z_copy(s, k).wait_send()
    for step in range(1, n):
        e_copy(step).wait_send()
    for t in range(row_tiles):
        out_copy(t).wait()
    gram_store(0, g1_hbm).wait()
    gram_store(1, g2_hbm).wait()


def finish(*refs):
    sources, targets, sem = refs[:3], refs[3:6], refs[6]
    copies = []
    for source, target in zip(sources, targets):
        pieces = 4 if source.shape[0] > 512 else 1
        size = source.shape[0] // pieces
        for p in range(pieces):
            span = pl.ds(p * size, size)
            copies.append(
                pltpu.make_async_copy(source.at[span], target.at[span], sem.at[len(copies)])
            )
    for copy in copies:
        copy.start()
    for copy in copies:
        copy.wait()


def per_device(n, n_col, snapshots, rotations):
    rows, width = snapshots.shape
    half = width // 2
    block = width // n
    groups = n // 2
    tiles = width // TILE
    symmetric = n == 8 and block == LANE
    units = len(UNITS) if symmetric else groups
    reach = TILE if symmetric else width
    owned = 4 if symmetric else 1
    sends = units if symmetric else max(groups - 1, tiles)
    bf16, f32, dma = jnp.bfloat16, jnp.float32, pltpu.SemaphoreType.DMA
    anywhere = pl.BlockSpec(memory_space=pl.ANY)
    shapes = (
        jax.ShapeDtypeStruct((block, width), f32),
        jax.ShapeDtypeStruct((block, width), f32),
        jax.ShapeDtypeStruct((rows, width), bf16),
    )
    results = pl.pallas_call(
        functools.partial(kernel, n, n_col),
        out_shape=shapes,
        in_specs=[anywhere] * 2,
        out_specs=(anywhere,) * 3,
        scratch_shapes=[
            pltpu.VMEM((rows, width), bf16),
            pltpu.VMEM((2, width, width), bf16),
            pltpu.VMEM((rows, half), bf16),
            pltpu.VMEM((rows, width), bf16),
            pltpu.VMEM((rows, width), f32),
            pltpu.VMEM((2, 2, units, block, reach), bf16),
            pltpu.VMEM((2, units, block, reach), bf16),
            pltpu.VMEM((2, units, block, reach), bf16),
            pltpu.VMEM((2, owned, groups - 1, block, reach), bf16),
            pltpu.VMEM((2, 4, 2, LANE, LANE), bf16),
            pltpu.VMEM((2, 4, 2, LANE, LANE), bf16),
            pltpu.VMEM((2, block, width), f32),
            pltpu.VMEM((1, width), f32),
            pltpu.VMEM((n - 1, 1, width), f32),
            pltpu.VMEM((rows, width), bf16),
            pltpu.VMEM((tiles, TILE, rows), bf16),
            dma((4,)),
            dma((half // TILE,)),
            dma((half // TILE,)),
            dma((2, sends)),
            dma((2, sends)),
            dma((2, sends)),
            dma((2, owned, groups - 1)),
            dma((2, 4, 2)),
            dma((2, 4, 2)),
            dma((n - 1,)),
            dma((n - 1,)),
            dma((2,)),
            dma((rows // TILE,)),
        ],
        compiler_params=pltpu.CompilerParams(
            collective_id=0, has_side_effects=True, vmem_limit_bytes=56 * 1024 * 1024
        ),
    )(snapshots, rotations)
    return pl.pallas_call(
        finish,
        out_shape=shapes,
        in_specs=[anywhere] * 3,
        out_specs=(anywhere,) * 3,
        scratch_shapes=[dma((12,))],
    )(*results)


def solution(mesh):
    return jax.shard_map(
        functools.partial(per_device, mesh.shape["row"], mesh.shape["col"]),
        mesh=mesh,
        in_specs=(P("row", "col"), P(None, "col", None)),
        out_specs=(P(("col", "row"), None), P(("col", "row"), None), P("row", "col")),
        check_vma=False,
    )
```

```python
import functools

import jax
import jax.numpy as jnp
from jax import lax
from jax.experimental import pallas as pl
from jax.experimental.pallas import tpu as pltpu
from jax.sharding import PartitionSpec as P

TILE = 256
LANE = 128

UNITS = ((0, 0), (0, 2), (0, 3), (0, 1), (2, 2), (2, 3), (2, 1), (3, 3), (3, 1), (1, 1))
FIRST = (0, 1, 2, 3, 4, 5, 6, 7, 8, 9)
STAGES = ((4, 5, 7), (0, 1, 2), (3, 6, 8, 9))


def kernel(
    n, n_col, x_hbm, rot_hbm, g1_hbm, g2_hbm, out_hbm,
    x, rot, left, pair, moved, part, peer, sums, landed, turn_out, turn_in,
    gram_out, energy, energy_in, shrunk,
    flipped, load_sem, left_send, left_recv, core_send, core_recv, z_send, z_recv,
    turn_send, turn_recv, e_send, e_recv, store_sem, shrunk_sem,
):
    rows, width = x.shape
    half = width // 2
    block = width // n
    groups = n // 2
    symmetric = n == 8 and block == LANE
    total_rows = rows * n
    tiles = width // TILE
    row_tiles = rows // TILE
    per_tile = TILE // (2 * block)

    me_col = lax.axis_index("col")
    me = lax.axis_index("row")
    core = lax.rem(me, 2)
    group = lax.div(me, 2)
    partner = me + 1 - 2 * core

    def peer_at(step):
        return lax.rem(me + step, n)

    load_x = pltpu.make_async_copy(x_hbm, x, load_sem.at[0])
    load_r0 = [
        pltpu.make_async_copy(
            rot_hbm.at[0, :, pl.ds(h * half, half)], rot.at[0, :, pl.ds(h * half, half)],
            load_sem.at[1 + h],
        )
        for h in range(2)
    ]
    load_r1 = pltpu.make_async_copy(rot_hbm.at[1], rot.at[1], load_sem.at[3])
    load_x.start()
    load_r0[0].start()
    load_r0[1].start()
    load_r1.start()

    following = lax.rem(me_col + 1, n_col)
    preceding = lax.rem(me_col + n_col - 1, n_col)
    barrier = pltpu.get_barrier_semaphore()
    for other in (following, preceding):
        pl.semaphore_signal(
            barrier, inc=1, device_id={"col": other, "row": me},
            device_id_type=pl.DeviceIdType.MESH,
        )
    for step in range(1, n):
        pl.semaphore_signal(
            barrier, inc=1, device_id={"col": me_col, "row": peer_at(step)},
            device_id_type=pl.DeviceIdType.MESH,
        )

    def remote(src, dst, send_sem, recv_sem, col, row):
        return pltpu.make_async_remote_copy(
            src_ref=src, dst_ref=dst, send_sem=send_sem, recv_sem=recv_sem,
            device_id={"col": col, "row": row}, device_id_type=pl.DeviceIdType.MESH,
        )

    def turn(into, first, column):
        def body(t, _):
            span = pl.ds(pl.multiple_of(t * TILE, TILE), TILE)
            into[span, pl.ds(column - first, TILE)] = jnp.dot(
                x[span, :], rot[0, :, pl.ds(column, TILE)], preferred_element_type=jnp.float32
            ).astype(jnp.bfloat16)
            return 0
        lax.fori_loop(0, row_tiles, body, 0)

    pieces = half // TILE
    left_copy = [
        remote(
            left.at[:, pl.ds(h * TILE, TILE)], pair.at[:, pl.ds(h * TILE, TILE)],
            left_send.at[h], left_recv.at[h], following, me,
        )
        for h in range(pieces)
    ]
    load_x.wait()
    load_r0[0].wait()
    turn(left, 0, 0)
    pl.semaphore_wait(barrier, n + 1)
    left_copy[0].start()

    def owned(u):
        g = UNITS[u][0]
        return [v for v in range(len(UNITS)) if UNITS[v][0] == g].index(u)

    def core_copy(s, u):
        return remote(
            part.at[s, 1 - core, u], peer.at[s, u],
            core_send.at[s, u], core_recv.at[s, u], me_col, partner,
        )

    def z_copy(s, u):
        g = UNITS[u][0] if symmetric else lax.rem(group + u, groups)
        k = lax.rem(g - group + 2 * groups - 1, groups)
        if symmetric:
            v = owned(u)
            return remote(
                sums.at[s, u], landed.at[s, v, k], z_send.at[s, u], z_recv.at[s, v, k],
                me_col, 2 * g + core,
            )
        return remote(
            sums.at[s, g], landed.at[s, 0, k], z_send.at[s, k], z_recv.at[s, 0, k],
            me_col, 2 * g + core,
        )

    def added(s, u):
        return part[s, core, u].astype(jnp.float32) + peer[s, u].astype(jnp.float32)

    def turn_copy(s, u, e):
        g, c = UNITS[u]
        return remote(
            turn_out.at[s, owned(u), e], turn_in.at[s, g, core],
            turn_send.at[s, owned(u), e], turn_recv.at[s, g, core], me_col, 2 * c + e,
        )

    def flip(source, g):
        flipped[g] = source[:, g * TILE:(g + 1) * TILE].T

    def pair_terms(s, source, units):
        for u in units:
            g, c = UNITS[u]
            term = jnp.dot(
                flipped[g], source[:, c * TILE:(c + 1) * TILE],
                preferred_element_type=jnp.float32,
            ).astype(jnp.bfloat16)
            part[s, 0, u] = term[:LANE]
            part[s, 1, u] = term[LANE:]
            core_copy(s, u).start()

    def pair_pass(s, units):
        for u in units:
            core_copy(s, u).wait_recv()

            @pl.when(group != UNITS[u][0])
            def _():
                sums[s, u] = added(s, u).astype(jnp.bfloat16)
                z_copy(s, u).start()

    def pair_sum(s, units):
        for u in units:
            g, c = UNITS[u]

            @pl.when(group == g)
            def _():
                v = owned(u)
                total = added(s, u)
                for k in range(groups - 1):
                    remote(
                        sums.at[s, u], landed.at[s, v, k], z_send.at[s, u], z_recv.at[s, v, k],
                        me_col, partner,
                    ).wait_recv()
                    total = total + landed[s, v, k].astype(jnp.float32)
                total = total / total_rows
                if c != g:
                    for e in range(2):
                        turn_out[s, v, e] = total[:, e * LANE:(e + 1) * LANE].T.astype(jnp.bfloat16)
                        turn_copy(s, u, e).start()
                gram_out[s, :, c * TILE:(c + 1) * TILE] = total

    def pair_turned(s, units):
        for u in units:
            g, c = UNITS[u]
            if c != g:

                @pl.when(group == c)
                def _():
                    for e in range(2):
                        remote(
                            turn_out.at[s, 0, 0], turn_in.at[s, g, e], turn_send.at[s, 0, 0],
                            turn_recv.at[s, g, e], me_col, partner,
                        ).wait_recv()
                        gram_out[s, :, (2 * g + e) * LANE:(2 * g + e + 1) * LANE] = turn_in[
                            s, g, e
                        ].astype(jnp.float32)

    def pair_drain(s, units):
        for u in units:
            g, c = UNITS[u]
            core_copy(s, u).wait_send()

            @pl.when(group != g)
            def _():
                z_copy(s, u).wait_send()

            if c != g:

                @pl.when(group == g)
                def _():
                    for e in range(2):
                        turn_copy(s, u, e).wait_send()

    def rows_copy(s, q):
        span = pl.ds(q * per_tile, per_tile)
        return remote(
            part.at[s, 1 - core, span], peer.at[s, span],
            core_send.at[s, q], core_recv.at[s, q], me_col, partner,
        )

    def rows_terms(s, source):
        def body(q, _):
            turned_tile = source[:, pl.ds(pl.multiple_of(q * TILE, TILE), TILE)].T
            for m in range(tiles):
                term = jnp.dot(
                    turned_tile, source[:, m * TILE:(m + 1) * TILE],
                    preferred_element_type=jnp.float32,
                ).astype(jnp.bfloat16)
                for e in range(2 * per_tile):
                    part[s, e % 2, q * per_tile + e // 2, :, m * TILE:(m + 1) * TILE] = term[
                        e * block:(e + 1) * block, :
                    ]
            rows_copy(s, q).start()
            return 0
        lax.fori_loop(0, tiles, body, 0)

    def rows_pass(s):
        for q in range(tiles):
            rows_copy(s, q).wait_recv()

        def body(k, _):
            g = lax.rem(group + k, groups)
            sums[s, g] = added(s, g).astype(jnp.bfloat16)
            z_copy(s, k).start()
            return 0
        lax.fori_loop(1, groups, body, 0)

    def rows_sum(s):
        total = added(s, group)
        for k in range(1, groups):
            z_copy(s, k).wait_recv()
            total = total + landed[s, 0, k - 1].astype(jnp.float32)
        gram_out[s] = total / total_rows

    def gram_store(s, target):
        return pltpu.make_async_copy(gram_out.at[s], target, store_sem.at[s])

    if symmetric:
        due = []
        for g in (0, 3, 2, 1):
            now = [u for u in FIRST if UNITS[u][0] == g]
            flip(x, g)
            pair_terms(0, x, now)
            pair_pass(0, due)
            due = now
    else:
        rows_terms(0, x)
    for h in range(1, pieces):
        turn(left, 0, h * TILE)
        left_copy[h].start()
    if symmetric:
        pair_pass(0, due)
    else:
        rows_pass(0)
    load_r0[1].wait()
    for h in range(pieces):
        turn(pair, 0, half + h * TILE)
    if symmetric:
        flip(pair, 2)
        flip(pair, 3)
        pair_terms(1, pair, STAGES[0])

    load_r1.wait()

    def add_moved(first, depth, fresh):
        def body(t, acc):
            span = pl.ds(pl.multiple_of(t * TILE, TILE), TILE)
            value = jnp.dot(
                pair[span, pl.ds(first, depth)], rot[1, pl.ds(first, depth), :],
                preferred_element_type=jnp.float32,
            )
            if not fresh:
                value = value + moved[span, :]
            moved[span, :] = value
            return acc + jnp.sum(value * value, axis=0, keepdims=True)
        return lax.fori_loop(0, row_tiles, body, jnp.zeros((1, width), jnp.float32))

    add_moved(half, half, True)
    if symmetric:
        pair_pass(1, STAGES[0])
    left_copy[0].wait_recv()
    if symmetric:
        flip(pair, 0)
        pair_terms(1, pair, STAGES[1])
    for h in range(pieces - 1):
        if h > 0:
            left_copy[h].wait_recv()
        add_moved(h * TILE, TILE, False)
    if symmetric:
        pair_pass(1, STAGES[1])
        pair_sum(0, FIRST)
        pair_turned(0, FIRST)
    else:
        rows_sum(0)
    gram_store(0, g1_hbm).start()
    if symmetric:
        pair_sum(1, STAGES[0])
    left_copy[pieces - 1].wait_recv()
    if symmetric:
        flip(pair, 1)
        pair_terms(1, pair, STAGES[2])
    else:
        rows_terms(1, pair)
    energy[...] = add_moved(half - TILE, TILE, False)

    def e_copy(step):
        return remote(
            energy, energy_in.at[step - 1], e_send.at[step - 1], e_recv.at[step - 1],
            me_col, peer_at(step),
        )

    for step in range(1, n):
        e_copy(step).start()
    if symmetric:
        pair_pass(1, STAGES[2])
        pair_sum(1, STAGES[1])
        pair_turned(1, STAGES[0] + STAGES[1])
    else:
        rows_pass(1)
    total = energy[...]
    for step in range(1, n):
        e_copy(step).wait_recv()
        total = total + energy_in[step - 1]
    singular = jnp.sqrt(total / total_rows + 1e-06)
    factor = jnp.maximum(singular - 1.8, 0.0) / singular

    def out_copy(t):
        span = pl.ds(pl.multiple_of(t * TILE, TILE), TILE)
        return pltpu.make_async_copy(shrunk.at[span, :], out_hbm.at[span, :], shrunk_sem.at[t])

    def shrink(t, _):
        span = pl.ds(pl.multiple_of(t * TILE, TILE), TILE)
        shrunk[span, :] = (moved[span, :] * factor).astype(jnp.bfloat16)
        out_copy(t).start()
        return 0

    lax.fori_loop(0, row_tiles, shrink, 0)
    if symmetric:
        pair_sum(1, STAGES[2])
        pair_turned(1, STAGES[2])
    else:
        rows_sum(1)
    gram_store(1, g2_hbm).start()

    for h in range(pieces):
        left_copy[h].wait_send()
    for s in range(2):
        if symmetric:
            pair_drain(s, FIRST)
        else:
            for q in range(tiles):
                rows_copy(s, q).wait_send()
            for k in range(1, groups):
                z_copy(s, k).wait_send()
    for step in range(1, n):
        e_copy(step).wait_send()
    for t in range(row_tiles):
        out_copy(t).wait()
    gram_store(0, g1_hbm).wait()
    gram_store(1, g2_hbm).wait()


def finish(*refs):
    sources, targets, held, load_sem, store_sem = refs[:3], refs[3:6], refs[6:9], refs[9], refs[10]
    loads, stores = [], []
    for source, target, room in zip(sources, targets, held):
        pieces = max(source.shape[0] // TILE, 1)
        size = source.shape[0] // pieces
        for p in range(pieces):
            span = pl.ds(p * size, size)
            at = len(loads)
            loads.append(pltpu.make_async_copy(source.at[span], room.at[span], load_sem.at[at]))
            stores.append(pltpu.make_async_copy(room.at[span], target.at[span], store_sem.at[at]))
    for load in loads:
        load.start()
    for load, store in zip(loads, stores):
        load.wait()
        store.start()
    for store in stores:
        store.wait()


def per_device(n, n_col, snapshots, rotations):
    rows, width = snapshots.shape
    half = width // 2
    block = width // n
    groups = n // 2
    tiles = width // TILE
    symmetric = n == 8 and block == LANE
    units = len(UNITS) if symmetric else groups
    reach = TILE if symmetric else width
    owned = 4 if symmetric else 1
    sends = units if symmetric else max(groups - 1, tiles)
    bf16, f32, dma = jnp.bfloat16, jnp.float32, pltpu.SemaphoreType.DMA
    anywhere = pl.BlockSpec(memory_space=pl.ANY)
    shapes = (
        jax.ShapeDtypeStruct((block, width), f32),
        jax.ShapeDtypeStruct((block, width), f32),
        jax.ShapeDtypeStruct((rows, width), bf16),
    )
    results = pl.pallas_call(
        functools.partial(kernel, n, n_col),
        out_shape=shapes,
        in_specs=[anywhere] * 2,
        out_specs=(anywhere,) * 3,
        scratch_shapes=[
            pltpu.VMEM((rows, width), bf16),
            pltpu.VMEM((2, width, width), bf16),
            pltpu.VMEM((rows, half), bf16),
            pltpu.VMEM((rows, width), bf16),
            pltpu.VMEM((rows, width), f32),
            pltpu.VMEM((2, 2, units, block, reach), bf16),
            pltpu.VMEM((2, units, block, reach), bf16),
            pltpu.VMEM((2, units, block, reach), bf16),
            pltpu.VMEM((2, owned, groups - 1, block, reach), bf16),
            pltpu.VMEM((2, 4, 2, LANE, LANE), bf16),
            pltpu.VMEM((2, 4, 2, LANE, LANE), bf16),
            pltpu.VMEM((2, block, width), f32),
            pltpu.VMEM((1, width), f32),
            pltpu.VMEM((n - 1, 1, width), f32),
            pltpu.VMEM((rows, width), bf16),
            pltpu.VMEM((tiles, TILE, rows), bf16),
            dma((4,)),
            dma((half // TILE,)),
            dma((half // TILE,)),
            dma((2, sends)),
            dma((2, sends)),
            dma((2, sends)),
            dma((2, owned, groups - 1)),
            dma((2, 4, 2)),
            dma((2, 4, 2)),
            dma((n - 1,)),
            dma((n - 1,)),
            dma((2,)),
            dma((rows // TILE,)),
        ],
        compiler_params=pltpu.CompilerParams(
            collective_id=0, has_side_effects=True, vmem_limit_bytes=56 * 1024 * 1024
        ),
    )(snapshots, rotations)
    return pl.pallas_call(
        finish,
        out_shape=shapes,
        in_specs=[anywhere] * 3,
        out_specs=(anywhere,) * 3,
        scratch_shapes=[pltpu.VMEM(shape.shape, shape.dtype) for shape in shapes]
        + [dma((2 + rows // TILE,))] * 2,
    )(*results)


def solution(mesh):
    return jax.shard_map(
        functools.partial(per_device, mesh.shape["row"], mesh.shape["col"]),
        mesh=mesh,
        in_specs=(P("row", "col"), P(None, "col", None)),
        out_specs=(P(("col", "row"), None), P(("col", "row"), None), P("row", "col")),
        check_vma=False,
    )
```

```python
import functools

import jax
import jax.numpy as jnp
from jax import lax
from jax.experimental import pallas as pl
from jax.experimental.pallas import tpu as pltpu
from jax.sharding import PartitionSpec as P

TILE = 256
LANE = 128

UNITS = ((0, 0), (0, 2), (0, 3), (0, 1), (2, 2), (2, 3), (2, 1), (3, 3), (3, 1), (1, 1))
FIRST = (0, 1, 2, 3, 4, 5, 6, 7, 8, 9)
STAGES = ((4, 5, 7), (0, 1, 2), (8, 3, 6, 9))


def kernel(
    n, n_col, x_hbm, rot_hbm, g1_hbm, g2_hbm, out_hbm,
    x, rot, left, pair, moved, part, peer, sums, landed, turn_out, turn_in,
    gram_out, energy, energy_in, shrunk,
    flipped, load_sem, left_send, left_recv, core_send, core_recv, z_send, z_recv,
    turn_send, turn_recv, e_send, e_recv, store_sem, shrunk_sem,
):
    rows, width = x.shape
    half = width // 2
    block = width // n
    groups = n // 2
    symmetric = n == 8 and block == LANE
    total_rows = rows * n
    tiles = width // TILE
    row_tiles = rows // TILE
    per_tile = TILE // (2 * block)

    me_col = lax.axis_index("col")
    me = lax.axis_index("row")
    core = lax.rem(me, 2)
    group = lax.div(me, 2)
    partner = me + 1 - 2 * core

    def peer_at(step):
        return lax.rem(me + step, n)

    load_x = pltpu.make_async_copy(x_hbm, x, load_sem.at[0])
    load_r0 = [
        pltpu.make_async_copy(
            rot_hbm.at[0, :, pl.ds(h * half, half)], rot.at[0, :, pl.ds(h * half, half)],
            load_sem.at[1 + h],
        )
        for h in range(2)
    ]
    load_r1 = pltpu.make_async_copy(rot_hbm.at[1], rot.at[1], load_sem.at[3])
    load_x.start()
    load_r0[0].start()
    load_r0[1].start()
    load_r1.start()

    following = lax.rem(me_col + 1, n_col)
    preceding = lax.rem(me_col + n_col - 1, n_col)
    barrier = pltpu.get_barrier_semaphore()
    for other in (following, preceding):
        pl.semaphore_signal(
            barrier, inc=1, device_id={"col": other, "row": me},
            device_id_type=pl.DeviceIdType.MESH,
        )
    for step in range(1, n):
        pl.semaphore_signal(
            barrier, inc=1, device_id={"col": me_col, "row": peer_at(step)},
            device_id_type=pl.DeviceIdType.MESH,
        )

    def remote(src, dst, send_sem, recv_sem, col, row):
        return pltpu.make_async_remote_copy(
            src_ref=src, dst_ref=dst, send_sem=send_sem, recv_sem=recv_sem,
            device_id={"col": col, "row": row}, device_id_type=pl.DeviceIdType.MESH,
        )

    def turn(into, first, column):
        def body(t, _):
            span = pl.ds(pl.multiple_of(t * TILE, TILE), TILE)
            into[span, pl.ds(column - first, TILE)] = jnp.dot(
                x[span, :], rot[0, :, pl.ds(column, TILE)], preferred_element_type=jnp.float32
            ).astype(jnp.bfloat16)
            return 0
        lax.fori_loop(0, row_tiles, body, 0)

    pieces = half // TILE
    left_copy = [
        remote(
            left.at[:, pl.ds(h * TILE, TILE)], pair.at[:, pl.ds(h * TILE, TILE)],
            left_send.at[h], left_recv.at[h], following, me,
        )
        for h in range(pieces)
    ]
    load_x.wait()
    load_r0[0].wait()
    turn(left, 0, 0)
    pl.semaphore_wait(barrier, n + 1)
    left_copy[0].start()

    def owned(u):
        g = UNITS[u][0]
        return [v for v in range(len(UNITS)) if UNITS[v][0] == g].index(u)

    def core_copy(s, u):
        return remote(
            part.at[s, 1 - core, u], peer.at[s, u],
            core_send.at[s, u], core_recv.at[s, u], me_col, partner,
        )

    def z_copy(s, u):
        g = UNITS[u][0] if symmetric else lax.rem(group + u, groups)
        k = lax.rem(g - group + 2 * groups - 1, groups)
        if symmetric:
            v = owned(u)
            return remote(
                sums.at[s, u], landed.at[s, v, k], z_send.at[s, u], z_recv.at[s, v, k],
                me_col, 2 * g + core,
            )
        return remote(
            sums.at[s, g], landed.at[s, 0, k], z_send.at[s, k], z_recv.at[s, 0, k],
            me_col, 2 * g + core,
        )

    def added(s, u):
        return part[s, core, u].astype(jnp.float32) + peer[s, u].astype(jnp.float32)

    def turn_copy(s, u, e):
        g, c = UNITS[u]
        return remote(
            turn_out.at[s, owned(u), e], turn_in.at[s, g, core],
            turn_send.at[s, owned(u), e], turn_recv.at[s, g, core], me_col, 2 * c + e,
        )

    def flip(source, g):
        flipped[g] = source[:, g * TILE:(g + 1) * TILE].T

    def pair_terms(s, source, units):
        for u in units:
            g, c = UNITS[u]
            term = jnp.dot(
                flipped[g], source[:, c * TILE:(c + 1) * TILE],
                preferred_element_type=jnp.float32,
            ).astype(jnp.bfloat16)
            part[s, 0, u] = term[:LANE]
            part[s, 1, u] = term[LANE:]
            core_copy(s, u).start()

    def pair_pass(s, units):
        for u in units:
            core_copy(s, u).wait_recv()

            @pl.when(group != UNITS[u][0])
            def _():
                sums[s, u] = added(s, u).astype(jnp.bfloat16)
                z_copy(s, u).start()

    def pair_sum(s, units):
        for u in units:
            g, c = UNITS[u]

            @pl.when(group == g)
            def _():
                v = owned(u)
                total = added(s, u)
                for k in range(groups - 1):
                    remote(
                        sums.at[s, u], landed.at[s, v, k], z_send.at[s, u], z_recv.at[s, v, k],
                        me_col, partner,
                    ).wait_recv()
                    total = total + landed[s, v, k].astype(jnp.float32)
                total = total / total_rows
                if c != g:
                    for e in range(2):
                        turn_out[s, v, e] = total[:, e * LANE:(e + 1) * LANE].T.astype(jnp.bfloat16)
                        turn_copy(s, u, e).start()
                gram_out[s, :, c * TILE:(c + 1) * TILE] = total

    def pair_turned(s, units):
        for u in units:
            g, c = UNITS[u]
            if c != g:

                @pl.when(group == c)
                def _():
                    for e in range(2):
                        remote(
                            turn_out.at[s, 0, 0], turn_in.at[s, g, e], turn_send.at[s, 0, 0],
                            turn_recv.at[s, g, e], me_col, partner,
                        ).wait_recv()
                        gram_out[s, :, (2 * g + e) * LANE:(2 * g + e + 1) * LANE] = turn_in[
                            s, g, e
                        ].astype(jnp.float32)

    def pair_drain(s, units):
        for u in units:
            g, c = UNITS[u]
            core_copy(s, u).wait_send()

            @pl.when(group != g)
            def _():
                z_copy(s, u).wait_send()

            if c != g:

                @pl.when(group == g)
                def _():
                    for e in range(2):
                        turn_copy(s, u, e).wait_send()

    def rows_copy(s, q):
        span = pl.ds(q * per_tile, per_tile)
        return remote(
            part.at[s, 1 - core, span], peer.at[s, span],
            core_send.at[s, q], core_recv.at[s, q], me_col, partner,
        )

    def rows_terms(s, source):
        def body(q, _):
            turned_tile = source[:, pl.ds(pl.multiple_of(q * TILE, TILE), TILE)].T
            for m in range(tiles):
                term = jnp.dot(
                    turned_tile, source[:, m * TILE:(m + 1) * TILE],
                    preferred_element_type=jnp.float32,
                ).astype(jnp.bfloat16)
                for e in range(2 * per_tile):
                    part[s, e % 2, q * per_tile + e // 2, :, m * TILE:(m + 1) * TILE] = term[
                        e * block:(e + 1) * block, :
                    ]
            rows_copy(s, q).start()
            return 0
        lax.fori_loop(0, tiles, body, 0)

    def rows_pass(s):
        for q in range(tiles):
            rows_copy(s, q).wait_recv()

        def body(k, _):
            g = lax.rem(group + k, groups)
            sums[s, g] = added(s, g).astype(jnp.bfloat16)
            z_copy(s, k).start()
            return 0
        lax.fori_loop(1, groups, body, 0)

    def rows_sum(s):
        total = added(s, group)
        for k in range(1, groups):
            z_copy(s, k).wait_recv()
            total = total + landed[s, 0, k - 1].astype(jnp.float32)
        gram_out[s] = total / total_rows

    def gram_store(s, target):
        return pltpu.make_async_copy(gram_out.at[s], target, store_sem.at[s])

    if symmetric:
        due = []
        for g in (0, 3, 2, 1):
            now = [u for u in FIRST if UNITS[u][0] == g]
            flip(x, g)
            pair_terms(0, x, now)
            pair_pass(0, due)
            due = now
    else:
        rows_terms(0, x)
    for h in range(1, pieces):
        turn(left, 0, h * TILE)
        left_copy[h].start()
    if symmetric:
        pair_pass(0, due)
    else:
        rows_pass(0)
    load_r0[1].wait()
    for h in range(pieces):
        turn(pair, 0, half + h * TILE)
    if symmetric:
        flip(pair, 2)
        flip(pair, 3)
        pair_terms(1, pair, STAGES[0])

    load_r1.wait()

    def add_moved(first, depth, fresh):
        def body(t, acc):
            span = pl.ds(pl.multiple_of(t * TILE, TILE), TILE)
            value = jnp.dot(
                pair[span, pl.ds(first, depth)], rot[1, pl.ds(first, depth), :],
                preferred_element_type=jnp.float32,
            )
            if not fresh:
                value = value + moved[span, :]
            moved[span, :] = value
            return acc + jnp.sum(value * value, axis=0, keepdims=True)
        return lax.fori_loop(0, row_tiles, body, jnp.zeros((1, width), jnp.float32))

    add_moved(half, half, True)
    if symmetric:
        pair_pass(1, STAGES[0])
    left_copy[0].wait_recv()
    if symmetric:
        flip(pair, 0)
        pair_terms(1, pair, STAGES[1])
        pair_pass(1, STAGES[1])
    for h in range(pieces - 1):
        if h > 0:
            left_copy[h].wait_recv()
        add_moved(h * TILE, TILE, False)
    if symmetric:
        pair_sum(0, FIRST)
        pair_turned(0, FIRST)
    else:
        rows_sum(0)
    gram_store(0, g1_hbm).start()
    if symmetric:
        pair_sum(1, STAGES[0])
    left_copy[pieces - 1].wait_recv()
    if symmetric:
        flip(pair, 1)
        pair_terms(1, pair, STAGES[2])
        pair_pass(1, STAGES[2])
    else:
        rows_terms(1, pair)
    energy[...] = add_moved(half - TILE, TILE, False)

    def e_copy(step):
        return remote(
            energy, energy_in.at[step - 1], e_send.at[step - 1], e_recv.at[step - 1],
            me_col, peer_at(step),
        )

    for step in range(1, n):
        e_copy(step).start()
    if symmetric:
        pair_sum(1, STAGES[1])
        pair_turned(1, STAGES[0] + STAGES[1])
    else:
        rows_pass(1)
    total = energy[...]
    for step in range(1, n):
        e_copy(step).wait_recv()
        total = total + energy_in[step - 1]
    singular = jnp.sqrt(total / total_rows + 1e-06)
    factor = jnp.maximum(singular - 1.8, 0.0) / singular

    def out_copy(t):
        span = pl.ds(pl.multiple_of(t * TILE, TILE), TILE)
        return pltpu.make_async_copy(shrunk.at[span, :], out_hbm.at[span, :], shrunk_sem.at[t])

    def shrink(t, _):
        span = pl.ds(pl.multiple_of(t * TILE, TILE), TILE)
        shrunk[span, :] = (moved[span, :] * factor).astype(jnp.bfloat16)
        out_copy(t).start()
        return 0

    lax.fori_loop(0, row_tiles, shrink, 0)
    if symmetric:
        pair_sum(1, STAGES[2])
        pair_turned(1, STAGES[2])
    else:
        rows_sum(1)
    gram_store(1, g2_hbm).start()

    for h in range(pieces):
        left_copy[h].wait_send()
    for s in range(2):
        if symmetric:
            pair_drain(s, FIRST)
        else:
            for q in range(tiles):
                rows_copy(s, q).wait_send()
            for k in range(1, groups):
                z_copy(s, k).wait_send()
    for step in range(1, n):
        e_copy(step).wait_send()
    for t in range(row_tiles):
        out_copy(t).wait()
    gram_store(0, g1_hbm).wait()
    gram_store(1, g2_hbm).wait()


def finish(*refs):
    sources, targets, held, load_sem, store_sem = refs[:3], refs[3:6], refs[6:9], refs[9], refs[10]
    loads, stores = [], []
    for source, target, room in zip(sources, targets, held):
        pieces = max(source.shape[0] // TILE, 1)
        size = source.shape[0] // pieces
        for p in range(pieces):
            span = pl.ds(p * size, size)
            at = len(loads)
            loads.append(pltpu.make_async_copy(source.at[span], room.at[span], load_sem.at[at]))
            stores.append(pltpu.make_async_copy(room.at[span], target.at[span], store_sem.at[at]))
    for load in loads:
        load.start()
    for load, store in zip(loads, stores):
        load.wait()
        store.start()
    for store in stores:
        store.wait()


def per_device(n, n_col, snapshots, rotations):
    rows, width = snapshots.shape
    half = width // 2
    block = width // n
    groups = n // 2
    tiles = width // TILE
    symmetric = n == 8 and block == LANE
    units = len(UNITS) if symmetric else groups
    reach = TILE if symmetric else width
    owned = 4 if symmetric else 1
    sends = units if symmetric else max(groups - 1, tiles)
    bf16, f32, dma = jnp.bfloat16, jnp.float32, pltpu.SemaphoreType.DMA
    anywhere = pl.BlockSpec(memory_space=pl.ANY)
    shapes = (
        jax.ShapeDtypeStruct((block, width), f32),
        jax.ShapeDtypeStruct((block, width), f32),
        jax.ShapeDtypeStruct((rows, width), bf16),
    )
    results = pl.pallas_call(
        functools.partial(kernel, n, n_col),
        out_shape=shapes,
        in_specs=[anywhere] * 2,
        out_specs=(anywhere,) * 3,
        scratch_shapes=[
            pltpu.VMEM((rows, width), bf16),
            pltpu.VMEM((2, width, width), bf16),
            pltpu.VMEM((rows, half), bf16),
            pltpu.VMEM((rows, width), bf16),
            pltpu.VMEM((rows, width), f32),
            pltpu.VMEM((2, 2, units, block, reach), bf16),
            pltpu.VMEM((2, units, block, reach), bf16),
            pltpu.VMEM((2, units, block, reach), bf16),
            pltpu.VMEM((2, owned, groups - 1, block, reach), bf16),
            pltpu.VMEM((2, 4, 2, LANE, LANE), bf16),
            pltpu.VMEM((2, 4, 2, LANE, LANE), bf16),
            pltpu.VMEM((2, block, width), f32),
            pltpu.VMEM((1, width), f32),
            pltpu.VMEM((n - 1, 1, width), f32),
            pltpu.VMEM((rows, width), bf16),
            pltpu.VMEM((tiles, TILE, rows), bf16),
            dma((4,)),
            dma((half // TILE,)),
            dma((half // TILE,)),
            dma((2, sends)),
            dma((2, sends)),
            dma((2, sends)),
            dma((2, owned, groups - 1)),
            dma((2, 4, 2)),
            dma((2, 4, 2)),
            dma((n - 1,)),
            dma((n - 1,)),
            dma((2,)),
            dma((rows // TILE,)),
        ],
        compiler_params=pltpu.CompilerParams(
            collective_id=0, has_side_effects=True, vmem_limit_bytes=56 * 1024 * 1024
        ),
    )(snapshots, rotations)
    return pl.pallas_call(
        finish,
        out_shape=shapes,
        in_specs=[anywhere] * 3,
        out_specs=(anywhere,) * 3,
        scratch_shapes=[pltpu.VMEM(shape.shape, shape.dtype) for shape in shapes]
        + [dma((2 + rows // TILE,))] * 2,
    )(*results)


def solution(mesh):
    return jax.shard_map(
        functools.partial(per_device, mesh.shape["row"], mesh.shape["col"]),
        mesh=mesh,
        in_specs=(P("row", "col"), P(None, "col", None)),
        out_specs=(P(("col", "row"), None), P(("col", "row"), None), P("row", "col")),
        check_vma=False,
    )
```
